256 devices in a mesh: ops: 16 (over z_lo, x, core), sec: 16 (over z_hi, y).
Axes of the slice: x: 4, y: 4, z: 8 (z_hi: 4, z_lo: 2; z = z_hi * 2 + z_lo), core: 2. Of those that a mesh axis runs over, the one named last changes fastest.
Arguments:
- wavefunction: float32 [16, 256, 1024], P('sec', 'ops'), may hold values from -8 to 8
- left_ops: float32 [16, 16, 256, 256], P('ops', 'sec'), may hold values from -0.375 to 0.375
- right_ops: float32 [16, 256, 256], P('ops'), may hold values from -0.375 to 0.375
- site_ops: float32 [16, 4, 4], P('ops'), may hold values from -3 to 3
- pattern: int32 [16, 16], P('ops', 'sec'), may hold values 0 or 1
- sector_sizes: int32 [16], P('sec'), may hold values from 1 to 256, 3072 in all
- owner: int32 [16], P('ops'), may hold values from 0 to 15
- slot: int32 [16], P('ops'), may hold values from 0 to 1
Outputs:
- basis: float32 [16, 256, 1024], P('sec', 'ops')
- complementary: float32 [16, 2, 256, 256], P('ops', None, 'sec')
The draws below stay inside these ranges and needn't reach their ends.
Inputs may be any that keep to these rules, and one draw needn't show every extreme that they name: `sector_sizes`: each sector has at least one live state; some sector has all 256.
All inputs are finite; a program needn't handle non-finite values. No bound on the sum of `pattern` or of `sector_sizes` on one device may be relied on, other than what follows from the above.
Results may differ from the reference program's by a relative error of at most 0.0003.
Values sent between devices are 32-bit elements; how exact they have to be, the bound alone decides.
No kernel may reach another device: no remote copies, remote signals or barrier semaphores. Data moves between devices by JAX's collectives and lax.ppermute only.
A program may use at most 64 MiB of HBM per device.

```python
import math
import jax
import jax.numpy as jnp
import numpy as np
from jax import lax

M = 256
C = 256
SLOTS = 2
OPS = 16
SEC = 16
N_OPS = 16


def draw_wavefunction(key, part):
    key_base = jax.random.fold_in(key, 11)
    key_sign = jax.random.fold_in(key, 12)
    key_common = jax.random.fold_in(key, 13)
    base_field = jax.random.normal(key_base, (SEC, M, 4 * C), jnp.float32)
    row_signs = jnp.where(jax.random.bernoulli(key_sign, 0.5, (SEC, M, 1)), 1.0, -1.0).astype(jnp.float32)
    common_row = jax.random.normal(key_common, (1, 1, 4 * C), jnp.float32)
    return jnp.clip(base_field + row_signs * common_row, -8.0, 8.0).astype(jnp.float32)


def set_ends(array, stream_key, low, high):
    index_at = [jax.random.randint(jax.random.fold_in(stream_key, axis), (), 0, length) for axis, length in enumerate(array.shape)]
    main_axis = array.shape.index(max(array.shape))
    neighbour = index_at[:main_axis] + [(index_at[main_axis] + 1) % array.shape[main_axis]] + index_at[main_axis + 1:]
    return array.at[tuple(index_at)].set(low).at[tuple(neighbour)].set(high)


def block_scale(stream_key, shape, shards, least, high):
    def one(position, parts):
        heights = jax.random.uniform(jax.random.fold_in(jax.random.fold_in(stream_key, 6), position), (parts,), jnp.float32, least / len(shards), high / len(shards))
        return jnp.repeat(jnp.exp(heights), shape[position] // parts).reshape((-1,) + (1,) * (len(shape) - position - 1))

    factor_of = one(*shards[0])
    for cut in shards[1:]:
        factor_of = factor_of * one(*cut)
    return factor_of


def rank_bounds(count, skew):
    weights = [(1 << 20) // math.isqrt(rank ** skew) + 1 for rank in range(1, count + 1)]
    scale = 1 + sum(weights) // (1 << 30)
    return np.cumsum(np.array([max(1, weight // scale) for weight in weights]))


def ranked(own_key, dims, count, slope):
    grid = rank_bounds(count, slope)
    pick = jax.random.randint(jax.random.fold_in(own_key, 1), dims, 0, int(grid[count - 1]))
    grade = jnp.searchsorted(jnp.asarray(grid, jnp.int32), pick, side="right")
    return jax.random.permutation(jax.random.fold_in(own_key, 2), count)[grade].astype(jnp.int32)


def length_profile(amount, total, limit, skew):
    loads = [(1 << 20) // math.isqrt(standing ** skew) + 1 for standing in range(2, amount + 1)]
    surplus, holding = total - limit - (amount - 1), [1] * (amount - 1)
    while surplus > 0:
        movable = [i for i in range(amount - 1) if holding[i] < limit]
        pool, budget = sum([loads[i] for i in movable]), surplus
        for i in movable:
            addition = min(limit - holding[i], max(1, budget * loads[i] // pool), surplus)
            holding[i] = holding[i] + addition
            surplus = surplus - addition
    return np.array([limit] + holding)


def ragged(own_key, number_of, total, limit, lean):
    if number_of == 2:
        one = jax.random.randint(own_key, (), max(1, total - limit), min(limit, total - 1) + 1)
        return jnp.stack([one, total - one])
    sizes = jnp.asarray(length_profile(number_of, total, limit, lean), jnp.int32)
    couples = (number_of - 1) // 2
    donor, sink = sizes[1:1 + 2 * couples:2], sizes[2:2 + 2 * couples:2]
    slack = jnp.minimum(donor - 1, limit - sink)
    passed = jax.random.randint(jax.random.fold_in(own_key, 1), (couples,), 0, 1 << 20) % (slack + 1)
    sizes = sizes.at[1:1 + 2 * couples:2].set(donor - passed).at[2:2 + 2 * couples:2].set(sink + passed)
    return sizes[jax.random.permutation(jax.random.fold_in(own_key, 2), number_of)]


def centred(stream_key, extent, deviation, bound, shards=(), kind=jnp.bfloat16):
    level = block_scale(stream_key, extent, shards, -0.22, 0.18) if shards else 1.0
    array = jax.random.normal(stream_key, extent, jnp.float32) * deviation * level
    return jnp.minimum(jnp.maximum(array, -bound), bound).astype(kind)


def setup_inputs(seed: int = 0) -> dict:
    key_list = jax.random.split(jax.random.key(seed), 9)
    wavefunction = draw_wavefunction(jax.random.fold_in(key_list[8], 71), 0)
    left_ops = centred(key_list[1], (OPS, SEC, M, M), M ** -0.5, 0.375, ((0, 16), (1, 16)), jnp.float32)
    right_ops = centred(key_list[2], (OPS, C, C), C ** -0.5, 0.375, ((0, 16),), jnp.float32)
    site_ops = centred(key_list[3], (OPS, 4, 4), 4 ** -0.5, 3.0, ((0, 16),), jnp.float32)
    pattern = set_ends((jax.random.randint(key_list[4], (OPS, SEC), 0, 4) < 3).astype(jnp.int32), jax.random.fold_in(key_list[4], 1), 0, 1)
    sector_sizes = ragged(key_list[5], SEC, SEC * M * 3 // 4, M, 2).astype(jnp.int32)
    owner = set_ends(ranked(key_list[6], (OPS,), N_OPS, 2), jax.random.fold_in(key_list[6], 3), 0, N_OPS - 1).astype(jnp.int32)
    slot = set_ends(jax.random.randint(key_list[7], (OPS,), 0, SLOTS), jax.random.fold_in(key_list[7], 1), 0, SLOTS - 1).astype(jnp.int32)
    return {"wavefunction": wavefunction, "left_ops": left_ops, "right_ops": right_ops, "site_ops": site_ops, "pattern": pattern, "sector_sizes": sector_sizes, "owner": owner, "slot": slot}


highest = lax.Precision.HIGHEST

def reference(wavefunction, left_ops, right_ops, site_ops, pattern, sector_sizes, owner, slot):
    sectors = wavefunction.shape[0]
    states = wavefunction.shape[1]
    columns = wavefunction.shape[2] // 4
    livemask = (jnp.arange(states, dtype=jnp.int32)[None, :] < sector_sizes[:, None]).astype(jnp.float32)
    source = (wavefunction * livemask[:, :, None]).reshape(sectors, states, 4, columns)
    blocks = left_ops * pattern[:, :, None, None].astype(jnp.float32)

    def apply_pair(accum, inputs):
        block, right, site = inputs
        mapped = jnp.einsum('smqc,cd->smqd', source, right, precision=highest)
        mapped = jnp.einsum('pq,smqd->smpd', site, mapped, precision=highest)
        return (accum + jnp.einsum('smn,snpd->smpd', block, mapped, precision=highest), None)
    start_value = jnp.zeros((sectors, states, 4, columns), jnp.float32)
    sigma, unused = lax.scan(apply_pair, start_value, (blocks, right_ops, site_ops))
    sigma = sigma * livemask[:, :, None, None]
    flat = sigma.reshape(sectors * states * 4, columns)
    gram = jnp.dot(flat.T.astype(jnp.float32), flat.astype(jnp.float32), precision=highest, preferred_element_type=jnp.float32)
    factor = jnp.linalg.cholesky(gram)
    ortho = jax.scipy.linalg.solve_triangular(factor, flat.T, lower=True).T
    scale = jnp.sqrt(jnp.float32(flat.shape[0]))
    basis = (ortho * scale).reshape(sectors, states, 4 * columns)
    frame = ortho.reshape(sectors, states, 4, columns)

    def renormalize(carry, inputs):
        block, site = inputs
        moved = jnp.einsum('smn,snqd->smqd', block, frame, precision=highest)
        moved = jnp.einsum('pq,smqd->smpd', site, moved, precision=highest)
        return (carry, jnp.einsum('smpc,smpd->cd', frame, moved, precision=highest))
    unused_carry, renorm = lax.scan(renormalize, jnp.zeros((), jnp.float32), (blocks, site_ops))
    target = owner * SLOTS + slot
    select = (target[:, None] == jnp.arange(N_OPS * SLOTS, dtype=jnp.int32)[None, :]).astype(jnp.float32)
    complementary = jnp.einsum('kj,kcd->jcd', select, renorm, precision=highest)
    return (basis, complementary.reshape(N_OPS, SLOTS, columns, columns))
```

```python
import functools

import jax
import jax.numpy as jnp
from jax import lax
from jax.experimental import pallas as pl
from jax.experimental.pallas import tpu as pltpu
from jax.sharding import PartitionSpec as P

SLOTS = 2
F32, BF16 = jnp.float32, jnp.bfloat16
HIGHEST = lax.Precision.HIGHEST
VM = pl.BlockSpec(memory_space=pltpu.VMEM)
SM = pl.BlockSpec(memory_space=pltpu.SMEM)

CORE = [(i, i ^ 1) for i in range(16)]
ZPAIR = [(i, i ^ 8) for i in range(16)]
XSHIFT = [[(i, (i & 9) | ((((i >> 1) + d) & 3) << 1)) for i in range(16)] for d in range(4)]


def other_z():
    pairs = []
    for i in range(16):
        step = 1 if i >> 3 else -1
        for s in range(16):
            t = ((((s >> 2) + step) & 3) << 2) | (s & 3)
            pairs.append((i * 16 + s, (i ^ 8) * 16 + t))
    return pairs


OTHER_Z = other_z()


def place():
    ops = lax.axis_index("ops")
    return ops, ops >> 3, (ops >> 1) & 3, ops & 1


def split(x):
    high = x.astype(BF16)
    return high, (x - high.astype(F32)).astype(BF16)


def dot3(a, b, dims=(((1,), (0,)), ((), ()))):
    def one(u, v):
        return lax.dot_general(u, v, dims, preferred_element_type=F32)

    return one(a[0], b[0]) + (one(a[0], b[1]) + one(a[1], b[0]))


NT = (((1,), (1,)), ((), ()))


def call(kernel, out, scratch, *args, specs=None, name=None):
    return pl.pallas_call(
        kernel,
        out_shape=out,
        in_specs=[VM] * len(args) if specs is None else specs,
        out_specs=jax.tree.map(lambda _: VM, out),
        scratch_shapes=scratch,
        compiler_params=pltpu.CompilerParams(vmem_limit_bytes=24 * 2**20),
        name=name,
    )(*args)


def gather(shard):
    pair = jnp.concatenate([shard, lax.ppermute(shard, "ops", ZPAIR)])
    mine = jnp.concatenate([pair, *[lax.ppermute(pair, "ops", XSHIFT[d]) for d in (1, 2, 3)]])
    return mine, lax.ppermute(mine, "ops", CORE)


def blocks(own, other, rows):
    _, z, x, c = place()
    for cc, ref in enumerate((own, other)):
        for d in range(4):
            for zz in range(2):
                index = ((z ^ zz) << 3) | (((x - d) & 3) << 1) | (c ^ cc)
                yield ref, (d * 2 + zz) * rows, index


def sigma_kernel(size, f, g, b0, b1, b2, b3, r0, r1, r2, r3, o0, o1, o2, o3, ph, pw, vh, vw, acc):
    _, z, x, c = place()
    live = size[0]
    row16 = lax.broadcasted_iota(jnp.int32, (16, 1024), 0)
    for ref, at, index in blocks(f, g, 16):
        first = pl.multiple_of(index * 16, 16)
        value = jnp.where(row16 + first < live, ref[at : at + 16, :], 0.0)
        high, low = split(value)
        ph[pl.ds(first, 16), :] = high
        pw[pl.ds(first, 16), :] = low
    pieces = [b[pl.ds(xx * 32 + pl.multiple_of(c * 16, 16), 16), :] for b in (b0, b1, b2, b3) for xx in range(4)]
    left = split(jnp.concatenate(pieces))
    u = dot3(left, (ph[...], pw[...]))
    for k, b in enumerate((b0, b1, b2, b3)):
        for p in range(4):
            total = None
            for q in range(4):
                term = b[128 + p : 129 + p, q : q + 1] * u[k * 64 : k * 64 + 64, q * 256 : q * 256 + 256]
                total = term if total is None else total + term
            high, low = split(total)
            vh[p * 64 : p * 64 + 64, k * 256 : k * 256 + 256] = high
            vw[p * 64 : p * 64 + 64, k * 256 : k * 256 + 256] = low
    right = split(jnp.concatenate([r[...] for r in (r0, r1, r2, r3)]))
    out = dot3((vh[...], vw[...]), right)
    at = lax.broadcasted_iota(jnp.int32, (256, 256), 0)
    m = z * 128 + ((at >> 4) & 3) * 32 + c * 16 + (at & 15)
    acc[...] = jnp.where(m < live, out, 0.0)
    for d, o in enumerate((o0, o1, o2, o3)):
        first = pl.multiple_of(((x + d) & 3) * 16, 16)
        for p in range(4):
            o[:, p * 256 : p * 256 + 256] = acc[pl.ds(p * 64 + first, 16), :]


def pair_kernel(f, g, left, site, out, xs, xh, xw, xt):
    ops, _, _, _ = place()
    for ref, at, index in blocks(f, g, 16):
        first = pl.multiple_of(index * 16, 16)
        value = ref[at : at + 16, :]
        xs[pl.ds(first, 16), :] = value
        high, low = split(value)
        xh[pl.ds(first, 16), :] = high
        xw[pl.ds(first, 16), :] = low
    y = dot3(split(left[...]), (xh[...], xw[...]))
    total, gram = jnp.zeros((256, 256), F32), jnp.zeros((16, 256), F32)
    first = pl.multiple_of(ops * 16, 16)
    for p in range(4):
        mixed = None
        for q in range(4):
            term = site[p, q] * y[:, q * 256 : q * 256 + 256]
            mixed = term if mixed is None else mixed + term
        x = xs[:, p * 256 : p * 256 + 256]
        xt[...] = x.T
        total = total + dot3(split(xt[...]), split(mixed))
        gram = gram + jnp.dot(xt[pl.ds(first, 16), :], x, precision=HIGHEST, preferred_element_type=F32)
    for s in range(16):
        out[s, :16, :] = total[s * 16 : s * 16 + 16, :]
        out[s, 16:, :] = gram


def route_kernel(f, g, gram, copies):
    ops, _, _, _ = place()
    slots = [jnp.zeros((16, 256), F32) for _ in range(SLOTS)]
    for ref, at, index in blocks(f, g, 40):
        gram[pl.ds(pl.multiple_of(index * 16, 16), 16), :] = ref[at + 16 : at + 32, :]
        target = ref[at + 32 : at + 33, :]
        for j in range(SLOTS):
            chosen = jnp.where(target == (ops * SLOTS + j).astype(F32), 1.0, 0.0)
            slots[j] = slots[j] + chosen * ref[at : at + 16, :]
    for s in range(16):
        for j in range(SLOTS):
            copies[s, j * 16 : j * 16 + 16, :] = slots[j]


def factor(block, size):
    count = size // 8
    lanes = lax.broadcasted_iota(jnp.int32, (8, 128), 1)
    sub = lax.broadcasted_iota(jnp.int32, (8, 128), 0)

    def spread(v):
        return jnp.broadcast_to(v, (8, 128))

    w = []
    for b in range(count):
        unit = jnp.where(lanes == sub + (size + b * 8), 1.0, 0.0)
        w.append(jnp.where(lanes < size, block[b * 8 : b * 8 + 8, :], unit))
    for b in range(count):
        t = b * 8
        col = [[spread(w[v][:, t + j : t + j + 1]) for j in range(8)] for v in range(b, count)]
        e = [[spread(col[0][j][i : i + 1, :]) if i >= j else None for j in range(8)] for i in range(8)]
        row = [spread(w[b][j : j + 1, :]) for j in range(8)]
        out = jnp.zeros((8, 128), F32)
        for j in range(8):
            inv = lax.rsqrt(e[j][j])
            row[j] = row[j] * inv
            out = jnp.where(sub == j, row[j], out)
            l = [e[i][j] * inv if i > j else None for i in range(8)]
            for i in range(j + 1, 8):
                for k in range(j + 1, i + 1):
                    e[i][k] = e[i][k] - l[i] * l[k]
            for i in range(j + 1, 8):
                row[i] = row[i] - l[i] * row[j]
            for v in range(1, count - b):
                col[v][j] = col[v][j] * inv
                for k in range(j + 1, 8):
                    col[v][k] = col[v][k] - l[k] * col[v][j]
        w[b] = out
        for v in range(1, count - b):
            rest = w[b + v]
            for j in range(8):
                rest = rest - col[v][j] * row[j]
            w[b + v] = rest
    return jnp.concatenate(w, 0)


def factor_kernel(a, x, scale, inverse, basis, u, v, size=64):
    v[...] = jnp.zeros_like(v)

    def dot(p, q):
        return jnp.dot(p, q, precision=HIGHEST, preferred_element_type=F32)

    for s in range(0, 256, size):
        low, high = s // 128 * 128, (s + size + 127) // 128 * 128
        pu = a[s : s + size, low:]
        at = [lax.broadcasted_iota(jnp.int32, (size, high), i) for i in (0, 1)]
        pv = jnp.where(at[1] == at[0] + s, 1.0, 0.0)
        if s:
            t = u[:s, low : low + 128].T[s - low : s - low + size, :]
            pu = pu - dot(t, u[:s, low:])
            pv = pv - dot(t, v[:s, :high])
        d = pu[:, :128]
        if s > low:
            d = pltpu.roll(d, 128 - (s - low), 1)
        m = pltpu.roll(factor(d, size), 128 - size, 1)[:, :size]
        u[s : s + size, low:] = dot(m, pu)
        v[s : s + size, :high] = dot(m, pv)
    inverse[...] = v[...]
    rows = jnp.concatenate([x[:, p * 256 : p * 256 + 256] for p in range(4)])
    q = dot3(split(rows), split(v[...]), NT) * scale
    for p in range(4):
        basis[:, p * 256 : p * 256 + 256] = q[p * 16 : p * 16 + 16, :]


def turn_kernel(arrived, inverse, out):
    sec = lax.axis_index("sec")
    rows = split(inverse[pl.ds(pl.multiple_of(sec * 16, 16), 16), :])
    turned = []
    for j in range(SLOTS):
        whole = jnp.concatenate([arrived[s, j * 16 : j * 16 + 16, :] for s in range(16)])
        turned.append(dot3(rows, split(whole)))
    result = dot3(split(jnp.concatenate(turned)), split(inverse[...]), NT)
    for j in range(SLOTS):
        out[j] = result[j * 16 : j * 16 + 16, :]


def body(wavefunction, left_ops, right_ops, site_ops, pattern, sector_sizes, owner, slot):
    def shape(*dims, dtype=F32):
        return jax.ShapeDtypeStruct(dims, dtype)

    def scratch(*dims, dtype=F32):
        return pltpu.VMEM(dims, dtype)

    def a2a(x, axis):
        return lax.all_to_all(x, axis, split_axis=0, concat_axis=0, tiled=True)

    z = lax.axis_index("ops") >> 3
    left, right = left_ops[0, 0], right_ops[0]
    site = site_ops[0] * pattern[0, 0].astype(F32)
    padded = jnp.pad(site, ((0, 4), (0, 252)))
    halves = left.reshape(2, 128, 256)
    kept = jnp.concatenate([lax.dynamic_index_in_dim(halves, z, 0, False), padded])
    given = jnp.concatenate([lax.dynamic_index_in_dim(halves, 1 - z, 0, False), padded])
    given = lax.ppermute(given, "ops", ZPAIR)
    right_z = lax.ppermute(right, ("ops", "sec"), OTHER_Z)
    mine, theirs = gather(wavefunction[0])
    lefts = [kept, given, lax.ppermute(kept, "ops", CORE), lax.ppermute(given, "ops", CORE)]
    rights = [right, right_z, lax.ppermute(right, "ops", CORE), lax.ppermute(right_z, "ops", CORE)]
    parts = call(
        sigma_kernel,
        [shape(16, 1024)] * 4,
        [scratch(256, 1024, dtype=BF16)] * 4 + [scratch(256, 256)],
        sector_sizes,
        mine,
        theirs,
        *lefts,
        *rights,
        specs=[SM] + [VM] * 10,
        name="sigma",
    )
    own = parts[0]
    for d in (1, 2, 3):
        own = own + lax.ppermute(parts[d], "ops", XSHIFT[d])
    mine, theirs = gather(own)
    pairs = call(
        pair_kernel,
        shape(16, 32, 256),
        [scratch(256, 1024)] + [scratch(256, 1024, dtype=BF16)] * 2 + [scratch(256, 256)],
        mine,
        theirs,
        left,
        site,
        specs=[VM, VM, VM, SM],
        name="pairs",
    )
    arrived = a2a(pairs, "sec").sum(axis=0)
    target = (owner[0] * SLOTS + slot[0]).astype(F32)
    mine, theirs = gather(jnp.concatenate([arrived, jnp.broadcast_to(target, (8, 256))]))
    gram, copies = call(route_kernel, [shape(256, 256), shape(16, 32, 256)], [], mine, theirs, name="route")
    routed = a2a(copies, "sec")
    total_rows = 4 * 256 * lax.axis_size("sec")
    inverse, basis = call(
        functools.partial(factor_outer, scale=float(total_rows) ** 0.5),
        [shape(256, 256), shape(16, 1024)],
        [scratch(256, 256), scratch(256, 256)],
        gram,
        own,
        name="factor",
    )
    out = call(turn_kernel, shape(2, 16, 256), [], routed, inverse, name="turn")
    return basis[None], out[None]


def factor_outer(a, x, inverse, basis, u, v, scale):
    factor_kernel(a, x, scale, inverse, basis, u, v)


def solution(mesh):
    placed = (
        P("sec", "ops", None),
        P("ops", "sec", None, None),
        P("ops", None, None),
        P("ops", None, None),
        P("ops", "sec"),
        P("sec"),
        P("ops"),
        P("ops"),
    )
    return jax.shard_map(
        body,
        mesh=mesh,
        in_specs=placed,
        out_specs=(P("sec", "ops", None), P("ops", None, "sec", None)),
        check_vma=False,
    )
```

```python
import functools

import jax
import jax.numpy as jnp
from jax import lax
from jax.experimental import pallas as pl
from jax.experimental.pallas import tpu as pltpu
from jax.sharding import PartitionSpec as P


SLOTS = 2
HALF = 4_000_000_000
F32, BF16 = jnp.float32, jnp.bfloat16
HIGHEST = lax.Precision.HIGHEST
VM = pl.BlockSpec(memory_space=pltpu.VMEM)
SM = pl.BlockSpec(memory_space=pltpu.SMEM)


def swap(mask):
    return [(i, i ^ mask) for i in range(16)]


CORE, ZPAIR = swap(1), swap(8)
NEAR = (1, 3, 2)


def exchange(parts, axis, unit):
    got = {}
    for d in NEAR:
        got[d] = lax.ppermute(parts[d], axis, swap(d * unit))
    return got


def other_z():
    pairs = []
    for i in range(16):
        step = 1 if i >> 3 else -1
        for s in range(16):
            t = ((((s >> 2) + step) & 3) << 2) | (s & 3)
            pairs.append((i * 16 + s, (i ^ 8) * 16 + t))
    return pairs


OTHER_Z = other_z()


def place():
    ops = lax.axis_index("ops")
    return ops, ops >> 3, (ops >> 1) & 3, ops & 1


def split(x):
    high = x.astype(BF16)
    return high, (x - high.astype(F32)).astype(BF16)


def dot3(a, b, dims=(((1,), (0,)), ((), ()))):
    def one(u, v):
        return lax.dot_general(u, v, dims, preferred_element_type=F32)

    return one(a[0], b[0]) + (one(a[0], b[1]) + one(a[1], b[0]))


NT = (((1,), (1,)), ((), ()))


def call(kernel, out, scratch, *args, specs=None, flops=0):
    return pl.pallas_call(
        kernel,
        out_shape=out,
        in_specs=[VM] * len(args) if specs is None else specs,
        out_specs=jax.tree.map(lambda _: VM, out),
        scratch_shapes=scratch,
        compiler_params=pltpu.CompilerParams(vmem_limit_bytes=24 * 2**20),
        cost_estimate=pl.CostEstimate(flops=flops or 200_000_000, bytes_accessed=1_000_000, transcendentals=0),
    )(*args)


def gather_pair(shard):
    return jnp.concatenate([shard, lax.ppermute(shard, "ops", ZPAIR)])


def gather_rest(pair):
    got = exchange([pair] * 4, "ops", 2)
    mine = jnp.concatenate([pair, got[1], got[2], got[3]])
    return mine, lax.ppermute(mine, "ops", CORE)


def blocks(own, other, rows):
    _, z, x, c = place()
    for cc, ref in enumerate((own, other)):
        for d in range(4):
            for zz in range(2):
                index = ((z ^ zz) << 3) | ((x ^ d) << 1) | (c ^ cc)
                yield ref, (d * 2 + zz) * rows, index


def prep_kernel(left, site, x, kept, given, copy):
    _, z, _, _ = place()
    low, high = left[:, :128], left[:, 128:]
    kept[:256, :] = jnp.where(z == 0, low, high)
    given[:256, :] = jnp.where(z == 0, high, low)
    kept[256:, :] = site[...]
    given[256:, :] = site[...]
    copy[...] = x[...]


def sigma_kernel(size, f, g, b0, b1, b2, b3, r0, r1, r2, r3, o0, o1, o2, o3, ph, pw, vh, vw, acc):
    _, z, x, c = place()
    live = size[0]
    row16 = lax.broadcasted_iota(jnp.int32, (16, 1024), 0)
    for cc, ref in enumerate((f, g)):
        for d in range(4):
            first = pl.multiple_of(((x ^ d) << 5) | ((c ^ cc) << 4), 16)
            value = jnp.where(row16 + (z * 128 + first) < live, ref[d * 16 : d * 16 + 16, :], 0.0)
            high, low = split(value)
            ph[pl.ds(first, 16), :] = high
            pw[pl.ds(first, 16), :] = low
    lefts = (b0, b1, b2, b3)
    pieces = [b[pl.ds(pl.multiple_of((i * 2 + c) * 16, 16), 16), :] for b in lefts for i in range(8)]
    u = dot3(split(jnp.concatenate(pieces)), (ph[...], pw[...]))
    for k, b in enumerate(lefts):
        for p in range(4):
            total = None
            for q in range(4):
                term = b[256 + p : 257 + p, q : q + 1] * u[k * 128 : k * 128 + 128, q * 256 : q * 256 + 256]
                total = term if total is None else total + term
            high, low = split(total)
            vh[p * 128 : p * 128 + 128, k * 256 : k * 256 + 256] = high
            vw[p * 128 : p * 128 + 128, k * 256 : k * 256 + 256] = low
    out = dot3((vh[...], vw[...]), split(jnp.concatenate([r[...] for r in (r0, r1, r2, r3)])))
    at = lax.broadcasted_iota(jnp.int32, (512, 256), 0)
    m = ((at >> 4) & 7) * 32 + c * 16 + (at & 15)
    acc[...] = jnp.where(m < live, out, 0.0)
    for d, o in enumerate((o0, o1, o2, o3)):
        for zz in range(2):
            first = ((z ^ zz) << 6) | ((x ^ d) << 4)
            for p in range(4):
                o[zz * 16 : zz * 16 + 16, p * 256 : p * 256 + 256] = acc[pl.ds(pl.multiple_of(p * 128 + first, 16), 16), :]


def sec_place():
    sec = lax.axis_index("sec")
    return sec, sec >> 2, sec & 3


def pair_kernel(f, g, left, site, o0, o1, o2, o3, xs, xh, xw, xt, acc):
    ops, _, _, _ = place()
    _, zh, y0 = sec_place()
    for ref, at, index in blocks(f, g, 16):
        first = pl.multiple_of(index * 16, 16)
        value = ref[at : at + 16, :]
        xs[pl.ds(first, 16), :] = value
        high, low = split(value)
        xh[pl.ds(first, 16), :] = high
        xw[pl.ds(first, 16), :] = low
    y = dot3(split(left[...]), (xh[...], xw[...]))
    total, gram = jnp.zeros((256, 256), F32), jnp.zeros((16, 256), F32)
    first = pl.multiple_of(ops * 16, 16)
    for p in range(4):
        mixed = None
        for q in range(4):
            term = site[p, q] * y[:, q * 256 : q * 256 + 256]
            mixed = term if mixed is None else mixed + term
        x = xs[:, p * 256 : p * 256 + 256]
        xt[...] = x.T
        total = total + dot3(split(xt[...]), split(mixed))
        gram = gram + jnp.dot(xt[pl.ds(first, 16), :], x, precision=HIGHEST, preferred_element_type=F32)
    acc[...] = total
    for d, o in enumerate((o0, o1, o2, o3)):
        for h in range(4):
            s = ((zh ^ h) << 2) | (y0 ^ d)
            o[h * 16 : h * 16 + 16, :] = acc[pl.ds(pl.multiple_of(s * 16, 16), 16), :]
        o[64:, :] = gram


def row_kernel(a, b, c, d, o0, o1, o2, o3):
    total = a[...] + b[...] + (c[...] + d[...])
    for h, o in enumerate((o0, o1, o2, o3)):
        o[:16, :] = total[h * 16 : h * 16 + 16, :]
        o[16:, :] = total[64:, :]


def route_kernel(f, g, gram, out, tmp):
    ops, _, _, _ = place()
    for ref, at, index in blocks(f, g, 40):
        gram[pl.ds(pl.multiple_of(index * 16, 16), 16), :] = ref[at + 16 : at + 32, :]
        tmp[pl.ds(pl.multiple_of(index * 24, 8), 16), :] = ref[at : at + 16, :]
        tmp[pl.ds(pl.multiple_of(index * 24, 8) + 16, 8), :] = ref[at + 32 : at + 40, :]
    for j in range(SLOTS):
        total = jnp.zeros((16, 256), F32)
        for k in range(16):
            target = tmp[k * 24 + 16 : k * 24 + 17, :]
            chosen = jnp.where(target == (ops * SLOTS + j).astype(F32), 1.0, 0.0)
            total = total + chosen * tmp[k * 24 : k * 24 + 16, :]
        out[j * 16 : j * 16 + 16, :] = total


def factor(block, size):
    count = size // 8
    lanes = lax.broadcasted_iota(jnp.int32, (8, 128), 1)
    sub = lax.broadcasted_iota(jnp.int32, (8, 128), 0)

    def spread(v):
        return jnp.broadcast_to(v, (8, 128))

    w = []
    for b in range(count):
        unit = jnp.where(lanes == sub + (size + b * 8), 1.0, 0.0)
        w.append(jnp.where(lanes < size, block[b * 8 : b * 8 + 8, :], unit))
    for b in range(count):
        t = b * 8
        col = [[spread(w[v][:, t + j : t + j + 1]) for j in range(8)] for v in range(b, count)]
        e = [[spread(col[0][j][i : i + 1, :]) if i >= j else None for j in range(8)] for i in range(8)]
        row = [spread(w[b][j : j + 1, :]) for j in range(8)]
        out = jnp.zeros((8, 128), F32)
        for j in range(8):
            inv = lax.rsqrt(e[j][j])
            row[j] = row[j] * inv
            out = jnp.where(sub == j, row[j], out)
            l = [e[i][j] * inv if i > j else None for i in range(8)]
            for i in range(j + 1, 8):
                for k in range(j + 1, i + 1):
                    e[i][k] = e[i][k] - l[i] * l[k]
            for i in range(j + 1, 8):
                row[i] = row[i] - l[i] * row[j]
            for v in range(1, count - b):
                col[v][j] = col[v][j] * inv
                for k in range(j + 1, 8):
                    col[v][k] = col[v][k] - l[k] * col[v][j]
        w[b] = out
        for v in range(1, count - b):
            rest = w[b + v]
            for j in range(8):
                rest = rest - col[v][j] * row[j]
            w[b + v] = rest
    return jnp.concatenate(w, 0)


def factor_steps(a, u, v, first, last, size=64):
    def dot(p, q):
        return jnp.dot(p, q, precision=HIGHEST, preferred_element_type=F32)

    for s in range(first, last, size):
        low, high = s // 128 * 128, (s + size + 127) // 128 * 128
        pu = a[s : s + size, low:]
        at = [lax.broadcasted_iota(jnp.int32, (size, high), i) for i in (0, 1)]
        pv = jnp.where(at[1] == at[0] + s, 1.0, 0.0)
        if s:
            t = u[:s, low : low + 128].T[s - low : s - low + size, :]
            pu = pu - dot(t, u[:s, low:])
            pv = pv - dot(t, v[:s, :high])
        d = pu[:, :128]
        if s > low:
            d = pltpu.roll(d, 128 - (s - low), 1)
        m = pltpu.roll(factor(d, size), 128 - size, 1)[:, :size]
        u[s : s + size, low:] = dot(m, pu)
        v[s : s + size, :high] = dot(m, pv)


def factor_first(a, u, v):
    factor_steps(a, u, v, 0, 128)


def factor_second(a, u0, v0, v, u):
    u[:128, :] = u0[...]
    v[:128, :128] = v0[...]
    v[:128, 128:] = jnp.zeros((128, 128), F32)
    factor_steps(a, u, v, 128, 256)


def basis_kernel(x, inverse, basis, scale):
    rows = jnp.concatenate([x[:, p * 256 : p * 256 + 256] for p in range(4)])
    q = dot3(split(rows), split(inverse[...]), NT) * scale
    for p in range(4):
        basis[:, p * 256 : p * 256 + 256] = q[p * 16 : p * 16 + 16, :]


def left_kernel(near, far, inverse, o0, o1, o2, o3, ch, cw, acc):
    _, zh, y0 = sec_place()
    ch[...] = jnp.zeros_like(ch)
    cw[...] = jnp.zeros_like(cw)
    for h, r, at in ((0, near, 0), (1, near, 32), (3, far, 0), (2, far, 32)):
        first = pl.multiple_of(((zh ^ h) << 6) | (y0 << 4), 16)
        for j in range(SLOTS):
            high, low = split(r[at + j * 16 : at + j * 16 + 16, :])
            ch[pl.ds(first, 16), j * 256 : j * 256 + 256] = high
            cw[pl.ds(first, 16), j * 256 : j * 256 + 256] = low
    rows = split(inverse[pl.ds(pl.multiple_of(zh * 64, 64), 64), :])
    acc[...] = dot3(rows, (ch[...], cw[...]))
    for d, o in enumerate((o0, o1, o2, o3)):
        first = pl.multiple_of((y0 ^ d) << 4, 16)
        for j in range(SLOTS):
            o[j * 16 : j * 16 + 16, :] = acc[pl.ds(first, 16), j * 256 : j * 256 + 256]


def right_kernel(a, b, c, d, inverse, out):
    total = a[...] + b[...] + (c[...] + d[...])
    result = dot3(split(total), split(inverse[...]), NT)
    for j in range(SLOTS):
        out[j] = result[j * 16 : j * 16 + 16, :]


def step(wavefunction, left_ops, right_ops, site_ops, pattern, sector_sizes, owner, slot):
    def shape(*dims, dtype=F32):
        return jax.ShapeDtypeStruct(dims, dtype)

    def scratch(*dims, dtype=F32):
        return pltpu.VMEM(dims, dtype)

    left, right = left_ops[0, 0], right_ops[0]
    site = site_ops[0] * pattern[0, 0].astype(F32)
    right_z = lax.ppermute(right, ("ops", "sec"), OTHER_Z)
    kept, given, shard = call(
        prep_kernel,
        [shape(264, 128), shape(264, 128), shape(16, 1024)],
        [],
        left,
        jnp.pad(site, ((0, 4), (0, 124))),
        wavefunction[0],
    )
    given = lax.ppermute(given, "ops", ZPAIR)
    got = exchange([wavefunction[0]] * 4, "ops", 2)
    mine = jnp.concatenate([shard, got[1], got[2], got[3]])
    parts = call(
        sigma_kernel,
        [shape(32, 1024)] * 4,
        [scratch(128, 1024, dtype=BF16)] * 2 + [scratch(512, 1024, dtype=BF16)] * 2 + [scratch(512, 256)],
        sector_sizes,
        mine,
        lax.ppermute(mine, "ops", CORE),
        kept,
        given,
        lax.ppermute(kept, "ops", CORE),
        lax.ppermute(given, "ops", CORE),
        right,
        right_z,
        lax.ppermute(right, "ops", CORE),
        lax.ppermute(right_z, "ops", CORE),
        specs=[SM] + [VM] * 10,
    )
    got = exchange(parts, "ops", 2)
    total = parts[0] + got[1] + (got[2] + got[3])
    other = lax.ppermute(total, "ops", ZPAIR)
    pair = jnp.concatenate([total[:16] + other[16:], total[16:] + other[:16]])
    own = pair[:16]
    parts = call(
        pair_kernel,
        [shape(80, 256)] * 4,
        [scratch(256, 1024)] + [scratch(256, 1024, dtype=BF16)] * 2 + [scratch(256, 256)] * 2,
        *gather_rest(pair),
        left,
        site,
        specs=[VM] * 3 + [SM],
    )
    got = exchange(parts, "sec", 1)
    parts = call(row_kernel, [shape(32, 256)] * 4, [], parts[0], got[1], got[2], got[3])
    got = exchange(parts, "sec", 4)
    arrived = parts[0] + got[1] + (got[2] + got[3])
    target = (owner[0] * SLOTS + slot[0]).astype(F32)
    packed = jnp.concatenate([arrived, jnp.broadcast_to(target, (8, 256))])
    gram, routed = call(
        route_kernel, [shape(256, 256), shape(32, 256)], [scratch(384, 256)], *gather_rest(gather_pair(packed))
    )
    other = lax.ppermute(routed, "sec", swap(4))
    upper, begun = call(factor_first, [shape(128, 256), shape(128, 128)], [], gram, flops=HALF)
    near, upper, begun = lax.optimization_barrier((jnp.concatenate([routed, other]), upper, begun))
    far = lax.ppermute(near, "sec", swap(12))
    inverse = call(factor_second, shape(256, 256), [scratch(256, 256)], gram, upper, begun, flops=HALF)
    parts = call(
        left_kernel, [shape(32, 256)] * 4, [scratch(256, 512, dtype=BF16)] * 2 + [scratch(64, 512)], near, far, inverse
    )
    got = exchange(parts, "sec", 1)
    total_rows = 4 * 256 * lax.axis_size("sec")
    basis = call(functools.partial(basis_kernel, scale=float(total_rows) ** 0.5), shape(16, 1024), [], own, inverse)
    out = call(right_kernel, shape(2, 16, 256), [], parts[0], got[1], got[2], got[3], inverse)
    return basis[None], out[None]


def solution(mesh):
    placed = (
        P("sec", "ops", None),
        P("ops", "sec", None, None),
        P("ops", None, None),
        P("ops", None, None),
        P("ops", "sec"),
        P("sec"),
        P("ops"),
        P("ops"),
    )
    return jax.shard_map(
        step,
        mesh=mesh,
        in_specs=placed,
        out_specs=(P("sec", "ops", None), P("ops", None, "sec", None)),
        check_vma=False,
    )
```

```python
import functools

import jax
import jax.numpy as jnp
from jax import lax
from jax.experimental import pallas as pl
from jax.experimental.pallas import tpu as pltpu
from jax.sharding import PartitionSpec as P


SLOTS = 2
HALF = 4_000_000_000
F32, BF16 = jnp.float32, jnp.bfloat16
HIGHEST = lax.Precision.HIGHEST
VM = pl.BlockSpec(memory_space=pltpu.VMEM)
SM = pl.BlockSpec(memory_space=pltpu.SMEM)


def swap(mask):
    return [(i, i ^ mask) for i in range(16)]


CORE, ZPAIR = swap(1), swap(8)
NEAR = (1, 3, 2)


def exchange(parts, axis, unit):
    got = {}
    for d in NEAR:
        got[d] = lax.ppermute(parts[d], axis, swap(d * unit))
    return got


def place():
    ops = lax.axis_index("ops")
    return ops, ops >> 3, (ops >> 1) & 3, ops & 1


def split(x):
    high = x.astype(BF16)
    return high, (x - high.astype(F32)).astype(BF16)


def dot3(a, b, dims=(((1,), (0,)), ((), ()))):
    def one(u, v):
        return lax.dot_general(u, v, dims, preferred_element_type=F32)

    return one(a[0], b[0]) + (one(a[0], b[1]) + one(a[1], b[0]))


NT = (((1,), (1,)), ((), ()))


def call(kernel, out, scratch, *args, specs=None, flops=0):
    return pl.pallas_call(
        kernel,
        out_shape=out,
        in_specs=[VM] * len(args) if specs is None else specs,
        out_specs=jax.tree.map(lambda _: VM, out),
        scratch_shapes=scratch,
        compiler_params=pltpu.CompilerParams(vmem_limit_bytes=24 * 2**20),
        cost_estimate=pl.CostEstimate(flops=flops or 200_000_000, bytes_accessed=1_000_000, transcendentals=0),
    )(*args)


def gather_pair(shard):
    return jnp.concatenate([shard, lax.ppermute(shard, "ops", ZPAIR)])


def gather_rest(pair):
    got = exchange([pair] * 4, "ops", 2)
    mine = jnp.concatenate([pair, got[1], got[2], got[3]])
    return mine, lax.ppermute(mine, "ops", CORE)


def blocks(own, other, rows):
    _, z, x, c = place()
    for cc, ref in enumerate((own, other)):
        for d in range(4):
            for zz in range(2):
                index = ((z ^ zz) << 3) | ((x ^ d) << 1) | (c ^ cc)
                yield ref, (d * 2 + zz) * rows, index


def prep_kernel(left, site, pattern, x, packed, copy):
    packed[:256, :] = left[...]
    row, lane = (lax.broadcasted_iota(jnp.int32, (8, 256), i) for i in (0, 1))
    values = jnp.zeros((8, 256), F32)
    scale = pattern[0, 0].astype(F32)
    for p in range(4):
        for q in range(4):
            values = jnp.where((row == p) & (lane == q), site[p, q] * scale, values)
    packed[256:, :] = values
    copy[...] = x[...]


def sigma_kernel(size, f, g, b0, b1, r0, r1, o0, o1, o2, o3, ph, pw, vh, vw, acc):
    _, z, x, c = place()
    live = size[0]
    row16 = lax.broadcasted_iota(jnp.int32, (16, 1024), 0)
    for ref, at, index in blocks(f, g, 16):
        first = pl.multiple_of(index * 16, 16)
        value = jnp.where(row16 + first < live, ref[at : at + 16, :], 0.0)
        high, low = split(value)
        ph[pl.ds(first, 16), :] = high
        pw[pl.ds(first, 16), :] = low
    lefts = (b0, b1)
    pieces = [b[pl.ds(pl.multiple_of((i * 2 + c) * 16, 16), 16), :] for b in lefts for i in range(8)]
    u = dot3(split(jnp.concatenate(pieces)), (ph[...], pw[...]))
    for k, b in enumerate(lefts):
        for p in range(4):
            total = None
            for q in range(4):
                term = b[256 + p : 257 + p, q : q + 1] * u[k * 128 : k * 128 + 128, q * 256 : q * 256 + 256]
                total = term if total is None else total + term
            high, low = split(total)
            vh[p * 128 : p * 128 + 128, k * 256 : k * 256 + 256] = high
            vw[p * 128 : p * 128 + 128, k * 256 : k * 256 + 256] = low
    out = dot3((vh[...], vw[...]), split(jnp.concatenate([r0[...], r1[...]])))
    at = lax.broadcasted_iota(jnp.int32, (512, 256), 0)
    m = ((at >> 4) & 7) * 32 + c * 16 + (at & 15)
    acc[...] = jnp.where(m < live, out, 0.0)
    for d, o in enumerate((o0, o1, o2, o3)):
        for zz in range(2):
            first = ((z ^ zz) << 6) | ((x ^ d) << 4)
            for p in range(4):
                o[zz * 16 : zz * 16 + 16, p * 256 : p * 256 + 256] = acc[pl.ds(pl.multiple_of(p * 128 + first, 16), 16), :]


def sec_place():
    sec = lax.axis_index("sec")
    return sec, sec >> 2, sec & 3


def pair_kernel(f, g, left, site, o0, o1, o2, o3, xs, xh, xw, xt, acc):
    ops, _, _, _ = place()
    _, zh, y0 = sec_place()
    for ref, at, index in blocks(f, g, 16):
        first = pl.multiple_of(index * 16, 16)
        value = ref[at : at + 16, :]
        xs[pl.ds(first, 16), :] = value
        high, low = split(value)
        xh[pl.ds(first, 16), :] = high
        xw[pl.ds(first, 16), :] = low
    y = dot3(split(left[...]), (xh[...], xw[...]))
    total, gram = jnp.zeros((256, 256), F32), jnp.zeros((16, 256), F32)
    first = pl.multiple_of(ops * 16, 16)
    for p in range(4):
        mixed = None
        for q in range(4):
            term = site[p, q] * y[:, q * 256 : q * 256 + 256]
            mixed = term if mixed is None else mixed + term
        at = slice(p * 256, p * 256 + 256)
        xt[...] = xs[:, at].T
        total = total + dot3(split(xt[...]), split(mixed))
        rows, right = split(xt[pl.ds(first, 16), :]), (xh[:, at], xw[:, at])
        low = jnp.dot(rows[1], right[1], preferred_element_type=F32)
        gram = gram + (dot3(rows, right) + low)
    acc[...] = total
    for d, o in enumerate((o0, o1, o2, o3)):
        for h in range(4):
            s = ((zh ^ h) << 2) | (y0 ^ d)
            o[h * 16 : h * 16 + 16, :] = acc[pl.ds(pl.multiple_of(s * 16, 16), 16), :]
        o[64:, :] = gram


def row_kernel(a, b, c, d, kept, given):
    total = a[...] + b[...] + (c[...] + d[...])
    for o, order in ((kept, (0, 3)), (given, (1, 2))):
        for n, h in enumerate(order):
            o[n * 16 : n * 16 + 16, :] = total[h * 16 : h * 16 + 16, :]
        o[32:, :] = total[64:, :]


def route_kernel(f, g, gram, out, tmp):
    ops, _, _, _ = place()
    for ref, at, index in blocks(f, g, 40):
        gram[pl.ds(pl.multiple_of(index * 16, 16), 16), :] = ref[at + 16 : at + 32, :]
        tmp[pl.ds(pl.multiple_of(index * 24, 8), 16), :] = ref[at : at + 16, :]
        tmp[pl.ds(pl.multiple_of(index * 24, 8) + 16, 8), :] = ref[at + 32 : at + 40, :]
    for j in range(SLOTS):
        total = jnp.zeros((16, 256), F32)
        for k in range(16):
            target = tmp[k * 24 + 16 : k * 24 + 17, :]
            chosen = jnp.where(target == (ops * SLOTS + j).astype(F32), 1.0, 0.0)
            total = total + chosen * tmp[k * 24 : k * 24 + 16, :]
        out[j * 16 : j * 16 + 16, :] = total


def factor(block, size):
    count = size // 8
    lanes = lax.broadcasted_iota(jnp.int32, (8, 128), 1)
    sub = lax.broadcasted_iota(jnp.int32, (8, 128), 0)

    def spread(v):
        return jnp.broadcast_to(v, (8, 128))

    w = []
    for b in range(count):
        unit = jnp.where(lanes == sub + (size + b * 8), 1.0, 0.0)
        w.append(jnp.where(lanes < size, block[b * 8 : b * 8 + 8, :], unit))
    for b in range(count):
        t = b * 8
        col = [[spread(w[v][:, t + j : t + j + 1]) for j in range(8)] for v in range(b, count)]
        e = [[spread(col[0][j][i : i + 1, :]) if i >= j else None for j in range(8)] for i in range(8)]
        row = [spread(w[b][j : j + 1, :]) for j in range(8)]
        out = jnp.zeros((8, 128), F32)
        for j in range(8):
            inv = lax.rsqrt(e[j][j])
            row[j] = row[j] * inv
            out = jnp.where(sub == j, row[j], out)
            l = [e[i][j] * inv if i > j else None for i in range(8)]
            for i in range(j + 1, 8):
                for k in range(j + 1, i + 1):
                    e[i][k] = e[i][k] - l[i] * l[k]
            for i in range(j + 1, 8):
                row[i] = row[i] - l[i] * row[j]
            for v in range(1, count - b):
                col[v][j] = col[v][j] * inv
                for k in range(j + 1, 8):
                    col[v][k] = col[v][k] - l[k] * col[v][j]
        w[b] = out
        for v in range(1, count - b):
            rest = w[b + v]
            for j in range(8):
                rest = rest - col[v][j] * row[j]
            w[b + v] = rest
    return jnp.concatenate(w, 0)


def factor_steps(a, u, v, first, last, size=64):
    def dot(p, q):
        return jnp.dot(p, q, precision=HIGHEST, preferred_element_type=F32)

    for s in range(first, last, size):
        low, high = s // 128 * 128, (s + size + 127) // 128 * 128
        pu = a[s : s + size, low:]
        at = [lax.broadcasted_iota(jnp.int32, (size, high), i) for i in (0, 1)]
        pv = jnp.where(at[1] == at[0] + s, 1.0, 0.0)
        if s:
            t = u[:s, low : low + 128].T[s - low : s - low + size, :]
            pu = pu - dot(t, u[:s, low:])
            pv = pv - dot(t, v[:s, :high])
        d = pu[:, :128]
        if s > low:
            d = pltpu.roll(d, 128 - (s - low), 1)
        m = pltpu.roll(factor(d, size), 128 - size, 1)[:, :size]
        u[s : s + size, low:] = dot(m, pu)
        v[s : s + size, :high] = dot(m, pv)


def factor_first(a, u, v):
    factor_steps(a, u, v, 0, 128)


def factor_second(a, u0, v0, v, u):
    u[:128, :] = u0[...]
    v[:128, :128] = v0[...]
    v[:128, 128:] = jnp.zeros((128, 128), F32)
    factor_steps(a, u, v, 128, 256)


def basis_kernel(x, inverse, basis, scale):
    rows = jnp.concatenate([x[:, p * 256 : p * 256 + 256] for p in range(4)])
    q = dot3(split(rows), split(inverse[...]), NT) * scale
    for p in range(4):
        basis[:, p * 256 : p * 256 + 256] = q[p * 16 : p * 16 + 16, :]


def left_kernel(near, far, inverse, o0, o1, o2, o3, ch, cw, acc):
    _, zh, y0 = sec_place()
    ch[...] = jnp.zeros_like(ch)
    cw[...] = jnp.zeros_like(cw)
    for h, r, at in ((0, near, 0), (1, near, 32), (3, far, 0), (2, far, 32)):
        first = pl.multiple_of(((zh ^ h) << 6) | (y0 << 4), 16)
        for j in range(SLOTS):
            high, low = split(r[at + j * 16 : at + j * 16 + 16, :])
            ch[pl.ds(first, 16), j * 256 : j * 256 + 256] = high
            cw[pl.ds(first, 16), j * 256 : j * 256 + 256] = low
    rows = split(inverse[pl.ds(pl.multiple_of(zh * 64, 64), 64), :])
    acc[...] = dot3(rows, (ch[...], cw[...]))
    for d, o in enumerate((o0, o1, o2, o3)):
        first = pl.multiple_of((y0 ^ d) << 4, 16)
        for j in range(SLOTS):
            o[j * 16 : j * 16 + 16, :] = acc[pl.ds(first, 16), j * 256 : j * 256 + 256]


def right_kernel(a, b, c, d, inverse, out):
    total = a[...] + b[...] + (c[...] + d[...])
    result = dot3(split(total), split(inverse[...]), NT)
    for j in range(SLOTS):
        out[j] = result[j * 16 : j * 16 + 16, :]


def step(wavefunction, left_ops, right_ops, site_ops, pattern, sector_sizes, owner, slot):
    def shape(*dims, dtype=F32):
        return jax.ShapeDtypeStruct(dims, dtype)

    def scratch(*dims, dtype=F32):
        return pltpu.VMEM(dims, dtype)

    left, right = left_ops[0, 0], right_ops[0]
    site = site_ops[0] * pattern[0, 0].astype(F32)
    other = lax.ppermute(wavefunction[0], "ops", ZPAIR)
    packed, shard = call(
        prep_kernel,
        [shape(264, 256), shape(16, 1024)],
        [],
        left,
        site_ops[0],
        pattern,
        wavefunction[0],
        specs=[VM, SM, SM, VM],
    )
    given = lax.ppermute(packed, "ops", CORE)
    right_given = lax.ppermute(right, "ops", CORE)
    pair = jnp.concatenate([shard, other])
    got = exchange([pair] * 4, "ops", 2)
    mine = jnp.concatenate([pair, got[1], got[2], got[3]])
    mine, given, right_given = lax.optimization_barrier((mine, given, right_given))
    parts = call(
        sigma_kernel,
        [shape(32, 1024)] * 4,
        [scratch(256, 1024, dtype=BF16)] * 2 + [scratch(512, 512, dtype=BF16)] * 2 + [scratch(512, 256)],
        sector_sizes,
        mine,
        lax.ppermute(mine, "ops", CORE),
        packed,
        given,
        right,
        right_given,
        specs=[SM] + [VM] * 6,
    )
    got = exchange(parts, "ops", 2)
    total = parts[0] + got[1] + (got[2] + got[3])
    other = lax.ppermute(total, "ops", ZPAIR)
    pair = jnp.concatenate([total[:16] + other[16:], total[16:] + other[:16]])
    own = pair[:16]
    parts = call(
        pair_kernel,
        [shape(80, 256)] * 4,
        [scratch(256, 1024)]
        + [scratch(256, 1024, dtype=BF16)] * 2
        + [scratch(256, 256)] * 2,
        *gather_rest(pair),
        left,
        site,
        specs=[VM] * 3 + [SM],
    )
    got = exchange(parts, "sec", 1)
    kept, given = call(row_kernel, [shape(48, 256)] * 2, [], parts[0], got[1], got[2], got[3])
    half = kept + lax.ppermute(given, "sec", swap(4))
    arrived = jnp.concatenate([half[:16], half[32:]]) + lax.ppermute(half[16:], "sec", swap(12))
    target = (owner[0] * SLOTS + slot[0]).astype(F32)
    packed = jnp.concatenate([arrived, jnp.broadcast_to(target, (8, 256))])
    gram, routed = call(
        route_kernel, [shape(256, 256), shape(32, 256)], [scratch(384, 256)], *gather_rest(gather_pair(packed))
    )
    other = lax.ppermute(routed, "sec", swap(4))
    upper, begun = call(factor_first, [shape(128, 256), shape(128, 128)], [], gram, flops=HALF)
    near, upper, begun = lax.optimization_barrier((jnp.concatenate([routed, other]), upper, begun))
    far = lax.ppermute(near, "sec", swap(12))
    inverse = call(factor_second, shape(256, 256), [scratch(256, 256)], gram, upper, begun, flops=HALF)
    parts = call(
        left_kernel, [shape(32, 256)] * 4, [scratch(256, 512, dtype=BF16)] * 2 + [scratch(64, 512)], near, far, inverse
    )
    got = exchange(parts, "sec", 1)
    total_rows = 4 * 256 * lax.axis_size("sec")
    basis = call(functools.partial(basis_kernel, scale=float(total_rows) ** 0.5), shape(16, 1024), [], own, inverse)
    out = call(right_kernel, shape(2, 16, 256), [], parts[0], got[1], got[2], got[3], inverse)
    return basis[None], out[None]


def solution(mesh):
    placed = (
        P("sec", "ops", None),
        P("ops", "sec", None, None),
        P("ops", None, None),
        P("ops", None, None),
        P("ops", "sec"),
        P("sec"),
        P("ops"),
        P("ops"),
    )
    return jax.shard_map(
        step,
        mesh=mesh,
        in_specs=placed,
        out_specs=(P("sec", "ops", None), P("ops", None, "sec", None)),
        check_vma=False,
    )
```

```python
import functools

import jax
import jax.numpy as jnp
from jax import lax
from jax.experimental import pallas as pl
from jax.experimental.pallas import tpu as pltpu
from jax.sharding import PartitionSpec as P


SLOTS = 2
HALF = 4_000_000_000
F32, BF16 = jnp.float32, jnp.bfloat16
HIGHEST = lax.Precision.HIGHEST
VM = pl.BlockSpec(memory_space=pltpu.VMEM)
SM = pl.BlockSpec(memory_space=pltpu.SMEM)


def swap(mask):
    return [(i, i ^ mask) for i in range(16)]


CORE, ZPAIR = swap(1), swap(8)
NEAR = (1, 3, 2)


BOTH = [(i * 16 + j, (i ^ 8) * 16 + (j ^ 12)) for i in range(16) for j in range(16)]


def exchange(parts, axis, unit):
    got = {}
    for d in NEAR:
        got[d] = lax.ppermute(parts[d], axis, swap(d * unit))
    return got


def place():
    ops = lax.axis_index("ops")
    return ops, ops >> 3, (ops >> 1) & 3, ops & 1


def split(x):
    high = x.astype(BF16)
    return high, (x - high.astype(F32)).astype(BF16)


def dot3(a, b, dims=(((1,), (0,)), ((), ()))):
    def one(u, v):
        return lax.dot_general(u, v, dims, preferred_element_type=F32)

    return one(a[0], b[0]) + (one(a[0], b[1]) + one(a[1], b[0]))


NT = (((1,), (1,)), ((), ()))


def call(kernel, out, scratch, *args, specs=None, flops=0):
    return pl.pallas_call(
        kernel,
        out_shape=out,
        in_specs=[VM] * len(args) if specs is None else specs,
        out_specs=jax.tree.map(lambda _: VM, out),
        scratch_shapes=scratch,
        compiler_params=pltpu.CompilerParams(vmem_limit_bytes=24 * 2**20),
        cost_estimate=pl.CostEstimate(flops=flops or 200_000_000, bytes_accessed=1_000_000, transcendentals=0),
    )(*args)


def gather_rest(pair):
    got = exchange([pair] * 4, "ops", 2)
    mine = jnp.concatenate([pair, got[1], got[2], got[3]])
    return mine, lax.ppermute(mine, "ops", CORE)


def blocks(own, other, rows):
    _, z, x, c = place()
    for cc, ref in enumerate((own, other)):
        for d in range(4):
            for zz in range(2):
                index = ((z ^ zz) << 3) | ((x ^ d) << 1) | (c ^ cc)
                yield ref, (d * 2 + zz) * rows, index


def prep_kernel(left, site, pattern, x, packed, copy):
    packed[:256, :] = left[...]
    row, lane = (lax.broadcasted_iota(jnp.int32, (8, 256), i) for i in (0, 1))
    values = jnp.zeros((8, 256), F32)
    scale = pattern[0, 0].astype(F32)
    for p in range(4):
        for q in range(4):
            values = jnp.where((row == p) & (lane == q), site[p, q] * scale, values)
    packed[256:, :] = values
    copy[...] = x[...]


def sigma_kernel(size, f, g, b0, b1, r0, r1, o0, o1, o2, o3, ph, pw, vh, vw, acc):
    _, z, x, c = place()
    live = size[0]
    row16 = lax.broadcasted_iota(jnp.int32, (16, 1024), 0)
    for ref, at, index in blocks(f, g, 16):
        first = pl.multiple_of(index * 16, 16)
        value = jnp.where(row16 + first < live, ref[at : at + 16, :], 0.0)
        high, low = split(value)
        ph[pl.ds(first, 16), :] = high
        pw[pl.ds(first, 16), :] = low
    lefts = (b0, b1)
    pieces = [b[pl.ds(pl.multiple_of((i * 2 + c) * 16, 16), 16), :] for b in lefts for i in range(8)]
    u = dot3(split(jnp.concatenate(pieces)), (ph[...], pw[...]))
    for k, b in enumerate(lefts):
        for p in range(4):
            total = None
            for q in range(4):
                term = b[256 + p : 257 + p, q : q + 1] * u[k * 128 : k * 128 + 128, q * 256 : q * 256 + 256]
                total = term if total is None else total + term
            high, low = split(total)
            vh[p * 128 : p * 128 + 128, k * 256 : k * 256 + 256] = high
            vw[p * 128 : p * 128 + 128, k * 256 : k * 256 + 256] = low
    out = dot3((vh[...], vw[...]), split(jnp.concatenate([r0[...], r1[...]])))
    at = lax.broadcasted_iota(jnp.int32, (512, 256), 0)
    m = ((at >> 4) & 7) * 32 + c * 16 + (at & 15)
    acc[...] = jnp.where(m < live, out, 0.0)
    for d, o in enumerate((o0, o1, o2, o3)):
        for zz in range(2):
            first = ((z ^ zz) << 6) | ((x ^ d) << 4)
            for p in range(4):
                o[zz * 16 : zz * 16 + 16, p * 256 : p * 256 + 256] = acc[pl.ds(pl.multiple_of(p * 128 + first, 16), 16), :]


def sec_place():
    sec = lax.axis_index("sec")
    return sec, sec >> 2, sec & 3


def pair_kernel(f, g, left, site, o0, o1, o2, o3, xs, xh, xw, xt, acc):
    ops, _, _, _ = place()
    _, zh, y0 = sec_place()
    for ref, at, index in blocks(f, g, 16):
        first = pl.multiple_of(index * 16, 16)
        value = ref[at : at + 16, :]
        xs[pl.ds(first, 16), :] = value
        high, low = split(value)
        xh[pl.ds(first, 16), :] = high
        xw[pl.ds(first, 16), :] = low
    y = dot3(split(left[...]), (xh[...], xw[...]))
    total, gram = jnp.zeros((256, 256), F32), jnp.zeros((16, 256), F32)
    first = pl.multiple_of(ops * 16, 16)
    for p in range(4):
        mixed = None
        for q in range(4):
            term = site[p, q] * y[:, q * 256 : q * 256 + 256]
            mixed = term if mixed is None else mixed + term
        at = slice(p * 256, p * 256 + 256)
        xt[...] = xs[:, at].T
        total = total + dot3(split(xt[...]), split(mixed))
        rows, right = split(xt[pl.ds(first, 16), :]), (xh[:, at], xw[:, at])
        low = jnp.dot(rows[1], right[1], preferred_element_type=F32)
        gram = gram + (dot3(rows, right) + low)
    acc[...] = total
    for d, o in enumerate((o0, o1, o2, o3)):
        for h in range(4):
            s = ((zh ^ h) << 2) | (y0 ^ d)
            o[h * 16 : h * 16 + 16, :] = acc[pl.ds(pl.multiple_of(s * 16, 16), 16), :]
        o[64:, :] = gram


def row_kernel(a, b, c, d, kept, given):
    total = a[...] + b[...] + (c[...] + d[...])
    for o, order in ((kept, (0, 3)), (given, (1, 2))):
        for n, h in enumerate(order):
            o[n * 16 : n * 16 + 16, :] = total[h * 16 : h * 16 + 16, :]
        o[32:, :] = total[64:, :]


def route_kernel(f, g, gram, out, tmp):
    ops, _, _, _ = place()
    for ref, at, index in blocks(f, g, 40):
        gram[pl.ds(pl.multiple_of(index * 16, 16), 16), :] = ref[at + 16 : at + 32, :]
        tmp[pl.ds(pl.multiple_of(index * 24, 8), 16), :] = ref[at : at + 16, :]
        tmp[pl.ds(pl.multiple_of(index * 24, 8) + 16, 8), :] = ref[at + 32 : at + 40, :]
    for j in range(SLOTS):
        total = jnp.zeros((16, 256), F32)
        for k in range(16):
            target = tmp[k * 24 + 16 : k * 24 + 17, :]
            chosen = jnp.where(target == (ops * SLOTS + j).astype(F32), 1.0, 0.0)
            total = total + chosen * tmp[k * 24 : k * 24 + 16, :]
        out[j * 16 : j * 16 + 16, :] = total


def factor(block, size):
    count = size // 8
    lanes = lax.broadcasted_iota(jnp.int32, (8, 128), 1)
    sub = lax.broadcasted_iota(jnp.int32, (8, 128), 0)

    def spread(v):
        return jnp.broadcast_to(v, (8, 128))

    w = []
    for b in range(count):
        unit = jnp.where(lanes == sub + (size + b * 8), 1.0, 0.0)
        w.append(jnp.where(lanes < size, block[b * 8 : b * 8 + 8, :], unit))
    for b in range(count):
        t = b * 8
        col = [[spread(w[v][:, t + j : t + j + 1]) for j in range(8)] for v in range(b, count)]
        e = [[spread(col[0][j][i : i + 1, :]) if i >= j else None for j in range(8)] for i in range(8)]
        row = [spread(w[b][j : j + 1, :]) for j in range(8)]
        out = jnp.zeros((8, 128), F32)
        for j in range(8):
            inv = lax.rsqrt(e[j][j])
            row[j] = row[j] * inv
            out = jnp.where(sub == j, row[j], out)
            l = [e[i][j] * inv if i > j else None for i in range(8)]
            for i in range(j + 1, 8):
                for k in range(j + 1, i + 1):
                    e[i][k] = e[i][k] - l[i] * l[k]
            for i in range(j + 1, 8):
                row[i] = row[i] - l[i] * row[j]
            for v in range(1, count - b):
                col[v][j] = col[v][j] * inv
                for k in range(j + 1, 8):
                    col[v][k] = col[v][k] - l[k] * col[v][j]
        w[b] = out
        for v in range(1, count - b):
            rest = w[b + v]
            for j in range(8):
                rest = rest - col[v][j] * row[j]
            w[b + v] = rest
    return jnp.concatenate(w, 0)


def factor_steps(a, u, v, first, last, size=64):
    def dot(p, q):
        return jnp.dot(p, q, precision=HIGHEST, preferred_element_type=F32)

    for s in range(first, last, size):
        low, high = s // 128 * 128, (s + size + 127) // 128 * 128
        pu = a[s : s + size, low:]
        at = [lax.broadcasted_iota(jnp.int32, (size, high), i) for i in (0, 1)]
        pv = jnp.where(at[1] == at[0] + s, 1.0, 0.0)
        if s:
            t = u[:s, low : low + 128].T[s - low : s - low + size, :]
            pu = pu - dot(t, u[:s, low:])
            pv = pv - dot(t, v[:s, :high])
        d = pu[:, :128]
        if s > low:
            d = pltpu.roll(d, 128 - (s - low), 1)
        m = pltpu.roll(factor(d, size), 128 - size, 1)[:, :size]
        u[s : s + size, low:] = dot(m, pu)
        v[s : s + size, :high] = dot(m, pv)


def factor_first(a, u, v):
    factor_steps(a, u, v, 0, 128)


def factor_second(a, u0, v0, v, u):
    u[:128, :] = u0[...]
    v[:128, :128] = v0[...]
    v[:128, 128:] = jnp.zeros((128, 128), F32)
    factor_steps(a, u, v, 128, 256)


def basis_kernel(x, inverse, basis, scale):
    rows = jnp.concatenate([x[:, p * 256 : p * 256 + 256] for p in range(4)])
    q = dot3(split(rows), split(inverse[...]), NT) * scale
    for p in range(4):
        basis[:, p * 256 : p * 256 + 256] = q[p * 16 : p * 16 + 16, :]


def left_kernel(near, far, inverse, o0, o1, o2, o3, ch, cw, acc):
    _, zh, y0 = sec_place()
    ch[...] = jnp.zeros_like(ch)
    cw[...] = jnp.zeros_like(cw)
    for h, r, at in ((0, near, 0), (1, near, 32), (3, far, 0), (2, far, 32)):
        first = pl.multiple_of(((zh ^ h) << 6) | (y0 << 4), 16)
        for j in range(SLOTS):
            high, low = split(r[at + j * 16 : at + j * 16 + 16, :])
            ch[pl.ds(first, 16), j * 256 : j * 256 + 256] = high
            cw[pl.ds(first, 16), j * 256 : j * 256 + 256] = low
    rows = split(inverse[pl.ds(pl.multiple_of(zh * 64, 64), 64), :])
    acc[...] = dot3(rows, (ch[...], cw[...]))
    for d, o in enumerate((o0, o1, o2, o3)):
        first = pl.multiple_of((y0 ^ d) << 4, 16)
        for j in range(SLOTS):
            o[j * 16 : j * 16 + 16, :] = acc[pl.ds(first, 16), j * 256 : j * 256 + 256]


def right_kernel(a, b, c, d, inverse, out):
    total = a[...] + b[...] + (c[...] + d[...])
    result = dot3(split(total), split(inverse[...]), NT)
    for j in range(SLOTS):
        out[j] = result[j * 16 : j * 16 + 16, :]


def step(wavefunction, left_ops, right_ops, site_ops, pattern, sector_sizes, owner, slot):
    def shape(*dims, dtype=F32):
        return jax.ShapeDtypeStruct(dims, dtype)

    def scratch(*dims, dtype=F32):
        return pltpu.VMEM(dims, dtype)

    left, right = left_ops[0, 0], right_ops[0]
    site = site_ops[0] * pattern[0, 0].astype(F32)
    other = lax.ppermute(wavefunction[0], "ops", ZPAIR)
    packed, shard = call(
        prep_kernel,
        [shape(264, 256), shape(16, 1024)],
        [],
        left,
        site_ops[0],
        pattern,
        wavefunction[0],
        specs=[VM, SM, SM, VM],
    )
    given = lax.ppermute(packed, "ops", CORE)
    right_given = lax.ppermute(right, "ops", CORE)
    pair = jnp.concatenate([shard, other])
    got = exchange([pair] * 4, "ops", 2)
    mine = jnp.concatenate([pair, got[1], got[2], got[3]])
    mine, given, right_given = lax.optimization_barrier((mine, given, right_given))
    parts = call(
        sigma_kernel,
        [shape(32, 1024)] * 4,
        [scratch(256, 1024, dtype=BF16)] * 2 + [scratch(512, 512, dtype=BF16)] * 2 + [scratch(512, 256)],
        sector_sizes,
        mine,
        lax.ppermute(mine, "ops", CORE),
        packed,
        given,
        right,
        right_given,
        specs=[SM] + [VM] * 6,
    )
    got = exchange(parts, "ops", 2)
    total = parts[0] + got[1] + (got[2] + got[3])
    other = lax.ppermute(total, "ops", ZPAIR)
    pair = jnp.concatenate([total[:16] + other[16:], total[16:] + other[:16]])
    own = pair[:16]
    parts = call(
        pair_kernel,
        [shape(80, 256)] * 4,
        [scratch(256, 1024)]
        + [scratch(256, 1024, dtype=BF16)] * 2
        + [scratch(256, 256)] * 2,
        *gather_rest(pair),
        left,
        site,
        specs=[VM] * 3 + [SM],
    )
    got = exchange(parts, "sec", 1)
    kept, given = call(row_kernel, [shape(48, 256)] * 2, [], parts[0], got[1], got[2], got[3])
    half = kept + lax.ppermute(given, "sec", swap(4))
    target = jnp.broadcast_to((owner[0] * SLOTS + slot[0]).astype(F32), (8, 256))
    own_rows = jnp.concatenate([half[:16], half[32:], target])
    peer_rows = lax.ppermute(own_rows, "ops", ZPAIR)
    owed = lax.ppermute(half[16:], "sec", swap(12))
    peer_owed = lax.ppermute(half[16:], ("ops", "sec"), BOTH)
    pair = jnp.concatenate([own_rows[:32] + owed, own_rows[32:], peer_rows[:32] + peer_owed, peer_rows[32:]])
    gram, routed = call(route_kernel, [shape(256, 256), shape(32, 256)], [scratch(384, 256)], *gather_rest(pair))
    other = lax.ppermute(routed, "sec", swap(4))
    upper, begun = call(factor_first, [shape(128, 256), shape(128, 128)], [], gram, flops=HALF)
    near, upper, begun = lax.optimization_barrier((jnp.concatenate([routed, other]), upper, begun))
    far = lax.ppermute(near, "sec", swap(12))
    inverse = call(factor_second, shape(256, 256), [scratch(256, 256)], gram, upper, begun, flops=HALF)
    parts = call(
        left_kernel, [shape(32, 256)] * 4, [scratch(256, 512, dtype=BF16)] * 2 + [scratch(64, 512)], near, far, inverse
    )
    got = exchange(parts, "sec", 1)
    total_rows = 4 * 256 * lax.axis_size("sec")
    basis = call(functools.partial(basis_kernel, scale=float(total_rows) ** 0.5), shape(16, 1024), [], own, inverse)
    out = call(right_kernel, shape(2, 16, 256), [], parts[0], got[1], got[2], got[3], inverse)
    return basis[None], out[None]


def solution(mesh):
    placed = (
        P("sec", "ops", None),
        P("ops", "sec", None, None),
        P("ops", None, None),
        P("ops", None, None),
        P("ops", "sec"),
        P("sec"),
        P("ops"),
        P("ops"),
    )
    return jax.shard_map(
        step,
        mesh=mesh,
        in_specs=placed,
        out_specs=(P("sec", "ops", None), P("ops", None, "sec", None)),
        check_vma=False,
    )
```
